32 devices in a mesh: seq: 8 (over z, y), cf: 2 (over x), fsdp: 2 (over core).
Axes of the slice: x: 2, y: 2, z: 4, core: 2. Of those that a mesh axis runs over, the one named last changes fastest.
Arguments:
- hidden_in: bfloat16 [8, 2, 512, 768], P('seq', 'cf', 'fsdp'), may hold values from -6 to 6
- clip_id: int32 [8, 2, 512], P('seq'), may hold values from 0 to 1, as said below
- w_qkv: bfloat16 [768, 2304], P(None, ('seq', 'cf', 'fsdp')), may hold values from -0.21875 to 0.21875
- w_out: bfloat16 [768, 768], P(('seq', 'cf', 'fsdp')), may hold values from -0.875 to 0.875
- w_fc: bfloat16 [768, 3072], P(None, ('seq', 'cf', 'fsdp')), may hold values from -0.21875 to 0.21875
- w_proj: bfloat16 [3072, 768], P(('seq', 'cf', 'fsdp')), may hold values from -0.109375 to 0.109375
- ln1_gain: bfloat16 [768], P(('seq', 'cf', 'fsdp')), may hold values from 0.5 to 1.5
- ln1_bias: bfloat16 [768], P(('seq', 'cf', 'fsdp')), may hold values from -2 to 2
- ln2_gain: bfloat16 [768], P(('seq', 'cf', 'fsdp')), may hold values from 0.5 to 1.5
- ln2_bias: bfloat16 [768], P(('seq', 'cf', 'fsdp')), may hold values from -2 to 2
- fc_bias: bfloat16 [3072], P(('seq', 'cf', 'fsdp')), may hold values from -3 to 3
- cotangent: bfloat16 [8, 2, 512, 768], P('seq', 'cf', 'fsdp'), may hold values from -6 to 6
Outputs:
- block_out: bfloat16 [8, 2, 512, 768], P('seq', 'cf', 'fsdp')
- input_grad: bfloat16 [8, 2, 512, 768], P('seq', 'cf', 'fsdp')
- grad_w_qkv: float32 [768, 2304], P(None, ('seq', 'cf', 'fsdp'))
- grad_w_out: float32 [768, 768], P(('seq', 'cf', 'fsdp'))
- grad_w_fc: float32 [768, 3072], P(None, ('seq', 'cf', 'fsdp'))
- grad_w_proj: float32 [3072, 768], P(('seq', 'cf', 'fsdp'))
- grad_ln1_gain: float32 [768], P(('seq', 'cf', 'fsdp'))
- grad_ln1_bias: float32 [768], P(('seq', 'cf', 'fsdp'))
- grad_ln2_gain: float32 [768], P(('seq', 'cf', 'fsdp'))
- grad_ln2_bias: float32 [768], P(('seq', 'cf', 'fsdp'))
- grad_fc_bias: float32 [3072], P(('seq', 'cf', 'fsdp'))
The draws below stay inside these ranges and needn't reach their ends.
Inputs may be any that keep to these rules, and one draw needn't show every extreme that they name: Along each half of a unit clip_id never falls and starts at 0; a unit holds one or two clips, unit 0 two; tokens of the two halves of a unit with the same number belong to one clip, and every clip has 512 tokens or more over both halves.
All inputs are finite; a program needn't handle non-finite values.
Results may differ from the reference program's by a relative error of at most 0.014.
Values may be sent and summed in bfloat16 or wider, within the bound.
A program may use at most 128 MiB of HBM per device.

```python
import jax
import jax.numpy as jnp
from jax import lax

D = 768
HEADS = 12
HEAD_DIM = 64
FF = 3072
CLIPS = 2
ROWS = 512
UNITS = 8


def draw_clip_id(key, part):
    count_key, cut_key = jax.random.split(key, 2)
    counts = jax.random.randint(count_key, (UNITS,), 1, CLIPS + 1).at[0].set(CLIPS)
    cut_rows = jax.random.randint(cut_key, (UNITS,), ROWS // 4, 3 * ROWS // 4 + 1)
    positions = jnp.arange(ROWS)
    active = (counts > 1)[:, None]
    context_ids = ((positions[None, :] >= cut_rows[:, None]) & active).astype(jnp.int32)
    future_ids = ((positions[None, :] >= (ROWS - cut_rows)[:, None]) & active).astype(jnp.int32)
    return jnp.stack([context_ids, future_ids], axis=1).astype(jnp.int32)


def steps_of(stream_key, shape, cuts, least, top_value):
    level = 1.0
    for dim, blocks in cuts:
        draws = jax.random.uniform(jax.random.fold_in(jax.random.fold_in(stream_key, 6), dim), (blocks,), jnp.float32, least / len(cuts), top_value / len(cuts))
        level = level * jnp.repeat(jnp.exp(draws), shape[dim] // blocks).reshape((-1,) + (1,) * (len(shape) - 1 - dim))
    return level


def gaussian(rng, dims, width, most, cuts=(), held_as=jnp.bfloat16):
    factor_of = steps_of(rng, dims, cuts, -0.22, 0.18) if cuts else 1.0
    values = jax.random.normal(rng, dims, jnp.float32) * width * factor_of
    return jnp.minimum(jnp.maximum(values, -most), most).astype(held_as)


def setup_inputs(seed: int = 0) -> dict:
    seeds = jax.random.split(jax.random.key(seed), 13)
    hidden_in = gaussian(seeds[0], (UNITS, 2, ROWS, D), 1.0, 6.0, ((0, 8), (1, 2), (2, 2)))
    clip_id = draw_clip_id(jax.random.fold_in(seeds[12], 71), 0)
    w_qkv = gaussian(seeds[2], (D, 3 * D), D ** -0.5, 0.21875, ((1, 32),))
    w_out = gaussian(seeds[3], (D, D), (D // 16) ** -0.5, 0.875, ((0, 32),))
    w_fc = gaussian(seeds[4], (D, FF), D ** -0.5, 0.21875, ((1, 32),))
    w_proj = gaussian(seeds[5], (FF, D), FF ** -0.5, 0.109375, ((0, 32),))
    ln1_gain = jnp.clip(1.0 + 0.1 * jax.random.normal(seeds[6], (D,), jnp.float32), 0.5, 1.5).astype(jnp.bfloat16)
    ln1_bias = gaussian(seeds[7], (D,), 0.3, 2.0, ((0, 32),))
    ln2_gain = jnp.clip(1.0 + 0.1 * jax.random.normal(seeds[8], (D,), jnp.float32), 0.5, 1.5).astype(jnp.bfloat16)
    ln2_bias = gaussian(seeds[9], (D,), 0.3, 2.0, ((0, 32),))
    fc_bias = gaussian(seeds[10], (FF,), 0.5, 3.0, ((0, 32),))
    cotangent = gaussian(seeds[11], (UNITS, 2, ROWS, D), 1.0, 6.0, ((0, 8), (1, 2), (2, 2)))
    return {"hidden_in": hidden_in, "clip_id": clip_id, "w_qkv": w_qkv, "w_out": w_out, "w_fc": w_fc, "w_proj": w_proj, "ln1_gain": ln1_gain, "ln1_bias": ln1_bias, "ln2_gain": ln2_gain, "ln2_bias": ln2_bias, "fc_bias": fc_bias, "cotangent": cotangent}


EPS = 1e-05
PRECISE = lax.Precision.HIGHEST

@jax.custom_vjp
def low(v):
    return lax.optimization_barrier(v.astype(jnp.bfloat16)).astype(jnp.float32)

@jax.custom_vjp
def low_back(v):
    return v

def low_keep(v):
    return (low(v), None)

def low_pass(kept, grad):
    return (grad,)

def back_keep(v):
    return (v, None)

def back_low(kept, grad):
    return (low(grad),)
low.defvjp(low_keep, low_pass)
low_back.defvjp(back_keep, back_low)

def norm_rows(values, gain, offset):
    center = values - lax.optimization_barrier(jnp.mean(values, axis=-1, keepdims=True))
    spread = lax.optimization_barrier(jnp.mean(center * center, axis=-1, keepdims=True))
    return center * lax.rsqrt(spread + EPS) * gain + offset

def gelu_tanh(values):
    return 0.5 * values * (1.0 + jnp.tanh(0.7978845608028654 * (values + 0.044715 * values * values * values)))

def project(left, right):
    return jnp.einsum('ntd,de->nte', left, right, precision=PRECISE)

def reference(hidden_in, clip_id, w_qkv, w_out, w_fc, w_proj, ln1_gain, ln1_bias, ln2_gain, ln2_bias, fc_bias, cotangent):
    unit_count = hidden_in.shape[0]
    length = 2 * hidden_in.shape[2]
    model_width = hidden_in.shape[3]
    score_scale = HEAD_DIM ** (-0.5)
    inputs = hidden_in.astype(jnp.float32).reshape(unit_count, length, model_width)
    unit_ids = clip_id.reshape(unit_count, length)
    positions = jnp.arange(length, dtype=jnp.int32)

    def attend_unit(block):
        packed, idents = block
        queries = packed[:, :model_width].reshape(length, HEADS, HEAD_DIM)
        keys = packed[:, model_width:2 * model_width].reshape(length, HEADS, HEAD_DIM)
        values = packed[:, 2 * model_width:].reshape(length, HEADS, HEAD_DIM)
        scores = low_back(jnp.einsum('qhd,khd->hqk', queries, keys, precision=PRECISE) * score_scale)
        allowed = (idents[:, None] == idents[None, :]) & (positions[None, :] <= positions[:, None])
        softmax_rows = low(jax.nn.softmax(jnp.where(allowed[None], scores, -1e+30), axis=-1))
        return jnp.einsum('hqk,khd->qhd', softmax_rows, values, precision=PRECISE).reshape(length, model_width)

    def forward(source, weight_qkv, weight_out, weight_fc, weight_proj, gain_one, bias_one, gain_two, bias_two, fc_shift):
        normed = low(norm_rows(source, gain_one, bias_one))
        packed = low(low_back(project(normed, weight_qkv)))
        attended = lax.map(jax.checkpoint(attend_unit), (packed, unit_ids))
        attended = low(low_back(attended))
        middle = source + low_back(project(attended, weight_out))
        normed_two = low(norm_rows(middle, gain_two, bias_two))
        before = low_back(project(normed_two, weight_fc) + fc_shift)
        activated = low(gelu_tanh(before))
        return middle + low_back(project(activated, weight_proj))
    result, pullback = jax.vjp(forward, inputs, w_qkv.astype(jnp.float32), w_out.astype(jnp.float32), w_fc.astype(jnp.float32), w_proj.astype(jnp.float32), ln1_gain.astype(jnp.float32), ln1_bias.astype(jnp.float32), ln2_gain.astype(jnp.float32), ln2_bias.astype(jnp.float32), fc_bias.astype(jnp.float32))
    grads = pullback(cotangent.astype(jnp.float32).reshape(unit_count, length, model_width))
    return (result.reshape(hidden_in.shape).astype(jnp.bfloat16), grads[0].reshape(hidden_in.shape).astype(jnp.bfloat16), grads[1], grads[2], grads[3], grads[4], grads[5], grads[6], grads[7], grads[8], grads[9])
```

```python
import jax
import jax.numpy as jnp
from jax import lax
from jax.experimental import pallas as pl
from jax.experimental.pallas import tpu as pltpu
from jax.sharding import PartitionSpec as P

HEADS = 12
HEAD_DIM = 64


EPS = 1e-05


def from_behind(block, axis, distance):
    devices = range(lax.axis_size(axis))
    route = [(i - distance, i) for i in devices if i - distance in devices]
    return lax.ppermute(block, axis, route)


def norm_rows(values, gain, offset):
    center = values - jnp.mean(values, axis=-1, keepdims=True)
    spread = jnp.mean(center * center, axis=-1, keepdims=True)
    return center * lax.rsqrt(spread + EPS) * gain + offset


def gelu_tanh(values):
    return (
        0.5
        * values
        * (1.0 + jnp.tanh(0.7978845608028654 * (values + 0.044715 * values * values * values)))
    )


def plain_dot(left, right):
    return jnp.dot(left, right, preferred_element_type=jnp.float32)


def inner_dot(left, right):
    return lax.dot_general(
        left, right, (((0,), (0,)), ((), ())), preferred_element_type=jnp.float32
    )


def outer_dot(left, right):
    return lax.dot_general(
        left, right, (((1,), (1,)), ((), ())), preferred_element_type=jnp.float32
    )


def split_heads(block):
    return block.reshape(block.shape[0], HEADS, HEAD_DIM).transpose(1, 0, 2)


def join_heads(block):
    return block.transpose(1, 0, 2).reshape(block.shape[1], -1)


def key_masks(clip_id, tok_rows):
    half_rows = clip_id.shape[2]
    side_index = lax.axis_index("cf")
    pair_index = lax.axis_index("fsdp")
    context_ids = clip_id[0, 0]
    future_ids = clip_id[0, 1]
    own_ids = jnp.where(side_index == 0, context_ids, future_ids)
    first_row = pair_index * tok_rows
    query_ids = lax.dynamic_slice_in_dim(own_ids, first_row, tok_rows)
    query_pos = first_row + jnp.arange(tok_rows, dtype=jnp.int32)
    key_pos = jnp.arange(half_rows, dtype=jnp.int32)
    remote = (query_ids[:, None] == context_ids[None, :]) & (side_index == 1)
    nearby = (query_ids[:, None] == own_ids[None, :]) & (key_pos[None, :] <= query_pos[:, None])
    return jnp.concatenate([remote, nearby], axis=1)


def attend(packed, allowed):
    model_width = packed.shape[1] // 3
    pair_kv = lax.all_gather(packed[:, model_width:], "fsdp", axis=0, tiled=True)
    remote_kv = from_behind(pair_kv, "cf", 1)
    key_rows = jnp.concatenate([remote_kv, pair_kv], axis=0)
    queries = split_heads(packed[:, :model_width])
    keys = split_heads(key_rows[:, :model_width])
    values = split_heads(key_rows[:, model_width:])
    score_scale = HEAD_DIM ** (-0.5)

    def one_head(operands):
        query_head, key_head, value_head = operands
        scores = jnp.where(allowed, outer_dot(query_head, key_head) * score_scale, -1e30)
        highest = jnp.max(scores, axis=1, keepdims=True)
        weights = jnp.exp(scores - highest)
        row_total = jnp.sum(weights, axis=1, keepdims=True)
        softmax_rows = (weights / row_total).astype(jnp.bfloat16)
        return (plain_dot(softmax_rows, value_head), (highest + jnp.log(row_total))[:, 0])

    mixed_heads, log_total = lax.map(one_head, (queries, keys, values))
    return (join_heads(mixed_heads).astype(jnp.bfloat16), log_total, key_rows)


def attend_back(packed, key_rows, log_total, attended_grad, allowed):
    model_width = packed.shape[1] // 3
    queries = split_heads(packed[:, :model_width])
    keys = split_heads(key_rows[:, :model_width])
    values = split_heads(key_rows[:, model_width:])
    grad_heads = split_heads(attended_grad)
    score_scale = HEAD_DIM ** (-0.5)

    def one_head(operands):
        query_head, key_head, value_head, log_head, grad_head = operands
        scores = outer_dot(query_head, key_head) * score_scale
        softmax_rows = jnp.where(allowed, jnp.exp(scores - log_head[:, None]), 0.0)
        rounded = softmax_rows.astype(jnp.bfloat16)
        prob_grad = outer_dot(grad_head, value_head)
        centre = jnp.sum(softmax_rows * prob_grad, axis=1, keepdims=True)
        score_grad = (softmax_rows * (prob_grad - centre)).astype(jnp.bfloat16)
        query_grad = plain_dot(score_grad, key_head) * score_scale
        key_grad = inner_dot(score_grad, query_head) * score_scale
        value_grad = inner_dot(rounded, grad_head)
        return (query_grad, key_grad, value_grad)

    query_grads, key_grads, value_grads = lax.map(
        one_head, (queries, keys, values, log_total, grad_heads)
    )
    return (
        join_heads(query_grads),
        jnp.concatenate([join_heads(key_grads), join_heads(value_grads)], axis=1),
    )


def forward_core(source, weights, allowed):
    (
        weight_qkv,
        weight_out,
        weight_fc,
        weight_proj,
        gain_one,
        bias_one,
        gain_two,
        bias_two,
        fc_shift,
    ) = weights
    normed = norm_rows(source, gain_one.astype(jnp.float32), bias_one.astype(jnp.float32)).astype(
        jnp.bfloat16
    )
    packed = plain_dot(normed, weight_qkv).astype(jnp.bfloat16)
    attended, log_total, key_rows = attend(packed, allowed)
    middle = source + plain_dot(attended, weight_out)
    normed_two = norm_rows(
        middle, gain_two.astype(jnp.float32), bias_two.astype(jnp.float32)
    ).astype(jnp.bfloat16)
    before = plain_dot(normed_two, weight_fc) + fc_shift.astype(jnp.float32)
    activated = gelu_tanh(before).astype(jnp.bfloat16)
    return (normed, packed, attended, log_total, key_rows, middle, normed_two, before, activated)


def split_dim(grad, axis_dim, outer_count, inner_count):
    pieces = grad.shape[axis_dim] // (outer_count * inner_count)
    return grad.reshape(
        grad.shape[:axis_dim] + (outer_count, inner_count, pieces) + grad.shape[axis_dim + 1 :]
    )


def merge_dims(part, axis_dim):
    return part.reshape(part.shape[:axis_dim] + (-1,) + part.shape[axis_dim + 2 :])


BF, F32 = jnp.bfloat16, jnp.float32
MESH = pl.DeviceIdType.MESH
BLK = 256
HALF = 128
D = 768
HEAD = 64

def nn(a, b):
    return lax.dot_general(a, b, (((1,), (0,)), ((), ())), preferred_element_type=F32)


def nt(a, b):
    return lax.dot_general(a, b, (((1,), (1,)), ((), ())), preferred_element_type=F32)


def tn(a, b):
    return lax.dot_general(a, b, (((0,), (0,)), ((), ())), preferred_element_type=F32)


def rows(start, size):
    return pl.ds(pl.multiple_of(start, 8), size)


def cols(start, size):
    return pl.ds(pl.multiple_of(start, 128), size)


def place():
    k, x, c = lax.axis_index("seq"), lax.axis_index("cf"), lax.axis_index("fsdp")
    return k, x, c, 2 * x + c


def unit_peer(k, x, c, i):
    return (k, 1 - x if i & 2 else x, 1 - c if i & 1 else c)


def group_peer(k, x, c, i):
    z, y = k // 2, k % 2
    s = lax.rem(jnp.int32(i) - 1, 3) + 1
    low = jnp.minimum(z, 3 - z)
    t = s - jnp.where((low == 1) & (s == 1), 1, 0)
    zi = jnp.where(z < 2, t, 3 - t)
    zi = jnp.where(jnp.int32(i) == 7, z, zi)
    yi = jnp.where(jnp.int32(i) >= 4, 1 - y, y)
    return zi * 2 + yi


def remote(src, dst, send, recv, dev):
    return pltpu.make_async_remote_copy(
        src_ref=src, dst_ref=dst, send_sem=send, recv_sem=recv, device_id=dev, device_id_type=MESH
    )


class GroupGather:
    def __init__(self, src, view, send, recv, local, relay=True):
        self.src, self.view, self.send, self.recv, self.local = src, view, send, recv, local
        self.k, self.x, self.c, _ = place()
        z = self.k // 2
        self.middle = (z == 1) | (z == 2)
        self.relay = relay
        self.y_dev = (group_peer(self.k, self.x, self.c, 7), self.x, self.c)

    def _peer(self, i):
        return (group_peer(self.k, self.x, self.c, i), self.x, self.c)

    def start_z(self):
        for i in (1, 2):
            remote(
                self.src, self.view(self.k), self.send.at[i - 1], self.recv.at[self.k], self._peer(i)
            ).start()

        def last():
            remote(
                self.src, self.view(self.k), self.send.at[2], self.recv.at[self.k], self._peer(3)
            ).start()

        if self.relay:
            pl.when(self.middle)(last)
        else:
            last()

    def start_y(self):
        mine = self.view(self.k)
        remote(self.src, mine, self.send.at[3], self.recv.at[self.k], self.y_dev).start()
        pltpu.make_async_copy(self.src, mine, self.local).start()

    def arrive(self, i):
        k = group_peer(self.k, self.x, self.c, i)
        blk = self.view(k)
        remote(blk, blk, self.send.at[0], self.recv.at[k], self.y_dev).wait_recv()
        return k

    def forward(self, step):
        i = step
        if self.relay:
            i = jnp.where(self.middle & (jnp.int32(step) >= 2), 5 - step, step)
        k = self.arrive(i)
        blk = self.view(k)
        remote(blk, blk, self.send.at[3 + i], self.recv.at[k], self.y_dev).start()
        if self.relay:
            @pl.when(self.middle & (jnp.int32(i) == 3))
            def _():
                remote(blk, blk, self.send.at[7], self.recv.at[k], self._peer(1)).start()
        return k

    def own(self):
        pltpu.make_async_copy(self.src, self.view(self.k), self.local).wait()

    def finish(self):
        for i in (7, 4, 5, 6):
            self.arrive(i)
        self.own()

    def drain(self):
        blk = self.view(self.k)

        def sent(i):
            remote(blk, blk, self.send.at[i], self.recv.at[self.k], self.y_dev).wait_send()

        for i in (0, 1, 3, 4, 5, 6):
            sent(i)

        def rest():
            sent(2)
            if self.relay:
                sent(7)

        if self.relay:
            pl.when(self.middle)(rest)
        else:
            rest()


class UnitGather:
    def __init__(self, view, send, recv):
        self.view, self.send, self.recv = view, send, recv
        self.k, self.x, self.c, self.m = place()

    def start(self, src=None):
        mine = self.view(self.m)
        src = mine if src is None else src
        for i in (2, 1):
            remote(
                src, mine, self.send.at[i], self.recv.at[0 if i == 1 else 1],
                unit_peer(self.k, self.x, self.c, i),
            ).start()

    def _other(self, i):
        return self.view(2 * (1 - self.x if i & 2 else self.x) + (1 - self.c if i & 1 else self.c))

    def _wait(self, i):
        blk = self._other(i)
        remote(
            blk, blk, self.send.at[0], self.recv.at[i - 1], unit_peer(self.k, self.x, self.c, 1)
        ).wait_recv()
        return blk

    def sibling(self):
        self._wait(1)

    def forward(self):
        blk = self._wait(2)
        remote(
            blk, blk, self.send.at[0], self.recv.at[2], unit_peer(self.k, self.x, self.c, 1)
        ).start()

    def finish(self):
        self._wait(3)

    def drain(self):
        blk = self.view(self.m)
        for i in range(3):
            remote(
                blk, blk, self.send.at[i], self.recv.at[0], unit_peer(self.k, self.x, self.c, 1)
            ).wait_send()


class GroupReduce:
    def __init__(self, src, n, yr, zs, zr, rl, sy, ry, sz, rz, rr):
        self.src, self.n, self.yr, self.zs, self.zr, self.rl = src, n, yr, zs, zr, rl
        self.sy, self.ry, self.sz, self.rz, self.rr = sy, ry, sz, rz, rr
        self.k, self.x, self.c, _ = place()
        self.z, self.y = self.k // 2, self.k % 2
        self.middle = (self.z == 1) | (self.z == 2)
        self.y_dev = (2 * self.z + 1 - self.y, self.x, self.c)

    def _blk(self, ref, b):
        return ref.at[rows(self.n * b, self.n)]

    def _turn(self, step):
        i = jnp.where(self.middle, step % 3 + 1, step)
        return i, group_peer(self.k, self.x, self.c, 4 - i) // 2

    def start(self, half):
        for q in range(2):
            end, mid = ((3 - q, 2 + q), (1 - q, q))[half]
            t = jnp.where(self.middle, mid, end)
            zz = jnp.where(self.z < 2, t, 3 - t)
            remote(
                self._blk(self.src, 2 * zz + 1 - self.y), self._blk(self.yr, zz),
                self.sy.at[2 * half + q], self.ry.at[zz], self.y_dev,
            ).start()

    def _landed(self, zz):
        blk = self._blk(self.yr, zz)
        remote(blk, blk, self.sy.at[0], self.ry.at[zz], self.y_dev).wait_recv()

    def pass_on(self, step):
        i, zz = self._turn(step)
        self._landed(zz)
        own = self.src[rows(self.n * (2 * zz + self.y), self.n), :].astype(F32)
        both = own + self.yr[rows(self.n * zz, self.n), :].astype(F32)
        here = self.zs.at[rows(self.n * (step - 1), self.n)]

        def straight():
            remote(
                here, self._blk(self.zr, self.z), self.sz.at[step - 1], self.rz.at[self.z],
                (2 * zz + self.y, self.x, self.c),
            ).start()

        if step == 2:
            here[...] = both.astype(BF)
            straight()
            return

        @pl.when(self.middle)
        def _():
            if step == 3:
                remote(self.rl, self.rl, self.sy.at[0], self.rr.at[0], self.y_dev).wait_recv()
                here[...] = (both + self.rl[...].astype(F32)).astype(BF)
            else:
                here[...] = both.astype(BF)
            straight()

        @pl.when(~self.middle)
        def _():
            here[...] = both.astype(BF)
            if step == 1:
                beside = group_peer(self.k, self.x, self.c, 1)
                remote(
                    here, self.rl, self.sz.at[0], self.rr.at[0], (beside, self.x, self.c)
                ).start()
            else:
                straight()

    def finish(self, out):
        self._landed(self.z)
        total = self.src[rows(self.n * self.k, self.n), :].astype(F32)
        total = total + self.yr[rows(self.n * self.z, self.n), :].astype(F32)

        def more(i):
            zz = group_peer(self.k, self.x, self.c, i) // 2
            blk = self._blk(self.zr, zz)
            remote(blk, blk, self.sz.at[0], self.rz.at[zz], self.y_dev).wait_recv()
            return self.zr[rows(self.n * zz, self.n), :].astype(F32)

        out[...] = total + more(1) + more(2)

        @pl.when(self.middle)
        def _():
            out[...] = out[...] + more(3)

    def drain(self):
        for i in range(4):
            blk = self._blk(self.yr, 0)
            remote(blk, blk, self.sy.at[i], self.ry.at[0], self.y_dev).wait_send()
        for i in range(3):
            blk = self._blk(self.zs, 0)
            remote(blk, blk, self.sz.at[i], self.rz.at[0], self.y_dev).wait_send()


class UnitReduce:
    def __init__(self, buf, send, recv):
        self.s1, self.s3, self.sx, self.r1, self.r3, self.rx = (buf.at[i] for i in range(6))
        self.send, self.recv = send, recv
        self.k, self.x, self.c, _ = place()
        self.sib = unit_peer(self.k, self.x, self.c, 1)
        self.far = unit_peer(self.k, self.x, self.c, 2)

    def give_own(self, v):
        self.s1[...] = v.astype(BF)
        remote(self.s1, self.r1, self.send.at[0], self.recv.at[0], self.sib).start()

    def give_far(self, v):
        self.s3[...] = v.astype(BF)
        remote(self.s3, self.r3, self.send.at[1], self.recv.at[1], self.sib).start()

    def cross(self, v):
        remote(self.r3, self.r3, self.send.at[1], self.recv.at[1], self.sib).wait_recv()
        self.sx[...] = (v + self.r3[...].astype(F32)).astype(BF)
        remote(self.sx, self.rx, self.send.at[2], self.recv.at[2], self.far).start()

    def arrive(self):
        remote(self.r1, self.r1, self.send.at[0], self.recv.at[0], self.sib).wait_recv()
        remote(self.rx, self.rx, self.send.at[2], self.recv.at[2], self.far).wait_recv()

    def rest(self, sl):
        return self.r1[sl, :].astype(F32) + self.rx[sl, :].astype(F32)

    def drain(self):
        for i in range(3):
            remote(self.s1, self.s1, self.send.at[i], self.recv.at[0], self.sib).wait_send()


def centred(v):
    c = v - jnp.mean(v, axis=-1, keepdims=True)
    r = lax.rsqrt(jnp.mean(c * c, axis=-1, keepdims=True) + EPS)
    return c, r


def lane_div(width, period):
    f = lax.broadcasted_iota(jnp.int32, (8, width), 1).astype(F32)
    return ((f + 0.5) * (1.0 / period)).astype(jnp.int32)


def spread(period):
    f = lax.broadcasted_iota(jnp.int32, (128, D), 1)
    i = lax.broadcasted_iota(jnp.int32, (128, D), 0)
    q = ((f.astype(F32) + 0.5) * (1.0 / period)).astype(jnp.int32)
    return ((f - q * period) == i).astype(BF)


def barrier(k, x, c):
    bar = pltpu.get_barrier_semaphore()
    for i in range(1, 8):
        pl.semaphore_signal(bar, inc=1, device_id=(group_peer(k, x, c, i), x, c), device_id_type=MESH)
    for i in (1, 2, 3):
        pl.semaphore_signal(bar, inc=1, device_id=unit_peer(k, x, c, i), device_id_type=MESH)
    pl.semaphore_wait(bar, 10)


def vectors_out(vec4, gv):
    _, _, _, m = place()
    flat = vec4[...].reshape(256, 128)
    wide = nn(flat, spread(24))
    lane = lane_div(D, 24)
    acc = jnp.zeros((8, D), F32)
    for j in range(32):
        mm, kk = j // 8, j % 8
        acc = acc + jnp.where(lane == 4 * kk + mm, wide[8 * j : 8 * j + 8, :], 0.0)
    gv[0:8, :] = acc
    mine = vec4[m].reshape(64, 128)
    wide = nn(mine, spread(96))
    lane = lane_div(D, 96)
    acc = jnp.zeros((8, D), F32)
    for kk in range(8):
        acc = acc + jnp.where(lane == kk, wide[8 * kk : 8 * kk + 8, :], 0.0)
    gv[8:16, :] = acc


def units_of(m, w):
    r = lax.rem(w - 3 * m + 16, 8)
    e = r // 4
    j = r - 4 * e
    return j, e


def block_at(qi, kj):
    return qi * (qi + 1) // 2 + kj


def attention_head(h, qt, bias, s_ref, e_ref, ot, inv_ref, give):
    q_all = (qt[HEAD * h : HEAD * h + HEAD, :].astype(F32) * 0.125).astype(BF)
    kt = qt[192 + HEAD * h : 192 + HEAD * h + HEAD, :]
    vt = qt[384 + HEAD * h : 384 + HEAD * h + HEAD, :]
    for qi in (3, 2, 1, 0):
        qs = slice(BLK * qi, BLK * qi + BLK)
        q = q_all[:, qs]
        top = None
        for kj in range(qi + 1):
            ks = slice(BLK * kj, BLK * kj + BLK)
            s = tn(kt[:, ks], q) + bias[block_at(qi, kj)]
            s_ref[ks, :] = s
            t = jnp.max(s, axis=0, keepdims=True)
            top = t if top is None else jnp.maximum(top, t)
        total = jnp.zeros((1, BLK), F32)
        acc = jnp.zeros((HEAD, BLK), F32)
        for kj in range(qi + 1):
            ks = slice(BLK * kj, BLK * kj + BLK)
            e = jnp.exp(s_ref[ks, :] - top)
            total = total + jnp.sum(e, axis=0, keepdims=True)
            low = e.astype(BF)
            e_ref[h, block_at(qi, kj)] = low
            acc = acc + nn(vt[:, ks], low)
        inv = 1.0 / total
        ot[HEAD * h : HEAD * h + HEAD, qs] = (acc * inv).astype(BF)
        inv_ref[h, :, qs] = inv
        give(h, qi)


def attention_back(h, qt, dot, e_ref, inv_ref, dp_ref, dk, dv, pgt):
    lo = HEAD * h
    q_all = (qt[lo : lo + HEAD, :].astype(F32) * 0.125).astype(BF)
    kt = qt[192 + lo : 192 + lo + HEAD, :]
    vt = qt[384 + lo : 384 + lo + HEAD, :]
    for qi in range(4):
        qs = slice(BLK * qi, BLK * qi + BLK)
        q = q_all[:, qs]
        inv = inv_ref[h, :, qs]
        do = (dot[lo : lo + HEAD, qs].astype(F32) * inv).astype(BF)
        centre = jnp.zeros((1, BLK), F32)
        for kj in range(qi + 1):
            ks = slice(BLK * kj, BLK * kj + BLK)
            dp = tn(vt[:, ks], do)
            centre = centre + jnp.sum(e_ref[h, block_at(qi, kj)].astype(F32) * dp, axis=0, keepdims=True)
            dp_ref[ks, :] = dp
        centre = centre * inv
        dq = jnp.zeros((HEAD, BLK), F32)
        for kj in range(qi + 1):
            ks = slice(BLK * kj, BLK * kj + BLK)
            e = e_ref[h, block_at(qi, kj)]
            ds = (e.astype(F32) * (dp_ref[ks, :] - centre)).astype(BF)
            gv_ = nt(do, e)
            gk_ = nt(q, ds)
            if kj == qi:
                dv[:, ks] = gv_
                dk[:, ks] = gk_
            else:
                dv[:, ks] = dv[:, ks] + gv_
                dk[:, ks] = dk[:, ks] + gk_
            dq = dq + nn(kt[:, ks], ds)
        pgt[lo : lo + HEAD, qs] = (dq * 0.125).astype(BF)
    pgt[192 + lo : 192 + lo + HEAD, :] = dk[...].astype(BF)
    pgt[384 + lo : 384 + lo + HEAD, :] = dv[...].astype(BF)


def norm_back(v, gain, grad):
    cc, r = centred(v)
    hat = cc * r
    t = grad * gain
    part = r * (
        t - jnp.mean(t, axis=-1, keepdims=True) - hat * jnp.mean(t * hat, axis=-1, keepdims=True)
    )
    return part, hat


def nt_two(a, b):
    high = a.astype(BF)
    low = (a - high.astype(F32)).astype(BF)
    return nt(high, b) + nt(low, b)


def flip(a, b):
    return a + b - 2 * a * b


def layer_kernel(
    hid, cot, clip, g1_in, b1_in, g2_in, b2_in, fb_in, wq_in, wo_in, fc_in, pj_in,
    block_out, in_grad, g_wq, g_wo, g_fc, g_pj, o_vec,
    mid, n2, norm, call, wq, wqh, wo, fc, pj, qt, at, inv_ref, ot, gv, bias, idr, e_ref, hat, vec4,
    vec_f, vec, hall, s_ref, dk, dv, act, db, slope, dmid, mid_out, far_part, part, mlow, agt, dot,
    pgt, gg, gs_pj, gs_fc, gs_wo, w48, wo_out, gh_q, gsw, gsy, gsz, gsr, ro_buf, rm_buf, ri_buf,
    go4, go_r, go_x, wo4, wo_far, wide, ex_r, ex_m, ex_g, yr_pj, zs_pj, zr_pj, rl_pj, rr_pj, sy_pj,
    ry_pj, sz_pj, rz_pj, yr_fc, zs_fc, zr_fc, rl_fc, rr_fc, sy_fc, ry_fc, sz_fc, rz_fc, yr_wo,
    zs_wo, zr_wo, rl_wo, rr_wo, sy_wo, ry_wo, sz_wo, rz_wo, sy_wq, ry_wq, sz_wq, rz_wq, vs, vr,
    vs2, vr2, hs, hr, qs, qr, os_, or_, fs, fr, ps, pr, us, ur, cs, cr, ns, nr, ro_s, ro_r, rm_s,
    rm_r, ri_s, ri_r, as_, ar, loc, in_s, os2, or2, wx_s, wx_r, gw_s, gw_r, ds_, dr_, xs, xr,
    go_s_sem, go_r_sem, es, er, es2, er2,
):
    k, x, c, m = place()
    barrier(k, x, c)
    pj_bufs = (yr_pj, zs_pj, zr_pj, rl_pj, sy_pj, ry_pj, sz_pj, rz_pj, rr_pj)
    fc_bufs = (yr_fc, zs_fc, zr_fc, rl_fc, sy_fc, ry_fc, sz_fc, rz_fc, rr_fc)
    wo_bufs = (yr_wo, zs_wo, zr_wo, rl_wo, sy_wo, ry_wo, sz_wo, rz_wo, rr_wo)
    gq = GroupGather(wq_in, lambda b: wq.at[rows(72 * b, 72)], qs, qr, loc.at[0], False)
    go = GroupGather(wo_in, lambda b: wo4.at[b, m], os_, or_, loc.at[1])
    gox = GroupGather(wo_far, lambda b: wo4.at[b, 2 * (1 - x) + c], os2, or2, loc.at[4])
    sib = unit_peer(k, x, c, 1)
    far = unit_peer(k, x, c, 2)
    gf = GroupGather(fc_in, lambda b: fc.at[rows(96 * b, 96)], fs, fr, loc.at[2])
    gp = GroupGather(pj_in, lambda b: pj.at[rows(96 * b, 96)], ps, pr, loc.at[3])
    gh = UnitGather(lambda b: hall.at[rows(BLK * b, BLK)], hs, hr)

    def spot(b, h):
        return rows(512 * (b // 2) + 256 * h + HALF * lax.rem(b, 2), HALF)

    gc = [UnitGather(lambda b, h=h: call.at[spot(b, h)], cs.at[h], cr.at[h]) for h in range(2)]
    gn = [UnitGather(lambda b, h=h: n2.at[spot(b, h)], ns.at[h], nr.at[h]) for h in range(2)]
    red_out = [UnitReduce(ro_buf.at[h], ro_s.at[h], ro_r.at[h]) for h in range(2)]
    red_mid = [UnitReduce(rm_buf.at[h], rm_s.at[h], rm_r.at[h]) for h in range(2)]
    red_in = [UnitReduce(ri_buf.at[h], ri_s.at[h], ri_r.at[h]) for h in range(2)]
    rs_pj = GroupReduce(gs_pj, 96, *pj_bufs)
    rs_fc = GroupReduce(gs_fc, 96, *fc_bufs)
    rs_wo = GroupReduce(gs_wo, 48, *wo_bufs)

    def unit_of(b, j):
        u = 12 * b + 3 * m + j
        return lax.rem(u // 8, 4), (u // 32) * 8 + lax.rem(u, 8)

    def send_rows(b, src):
        for j in range(3):
            g, slot = unit_of(b, j)
            part = src.at[24 * j : 24 * j + 24] if src is wq_in else src.at[rows(72 * b + 24 * j, 24)]
            dst = wqh.at[rows(24 * slot, 24)]

            @pl.when(g == m)
            def _():
                pltpu.make_async_copy(part, dst, ur.at[slot]).start()

            @pl.when(g != m)
            def _():
                remote(part, dst, us.at[3 * b + j], ur.at[slot], (k, g // 2, lax.rem(g, 2))).start()

    vec_f[...] = jnp.zeros((8, 128), F32)
    for r_, v_in in enumerate((g1_in, b1_in, g2_in, b2_in)):
        vec_f[r_ : r_ + 1, 0:24] = v_in[...].astype(F32)
    vec_f[4:5, 0:96] = fb_in[...].astype(F32)
    vec[...] = vec_f[...].astype(BF)
    for i in range(1, 8):
        kk = group_peer(k, x, c, i)
        remote(vec, vec4.at[m, k], vs.at[i - 1], vr.at[k], (kk, x, c)).start()
    wo_move = remote(wo_in, wo_far, wx_s.at[0], wx_r.at[0], far)
    wo_move.start()
    gh.start(hid)
    gq.start_z()
    gq.start_y()
    go.start_y()
    send_rows(k, wq_in)
    vec4[m, k] = vec[...]
    own_in = [pltpu.make_async_copy(hid, hall.at[rows(BLK * m, BLK)], in_s.at[0])] + [
        pltpu.make_async_copy(cot.at[HALF * h : HALF * h + HALF], call.at[spot(m, h)], in_s.at[1 + h])
        for h in range(2)
    ]
    for copy in own_in:
        copy.start()
    for half in range(2):
        idr[:, 512 * half : 512 * half + 512] = jnp.broadcast_to(
            clip[half : half + 1, :].astype(F32), (8, 512)
        )
    for kj in range(4):
        across = jnp.broadcast_to(idr[0:1, BLK * kj : BLK * kj + BLK], (BLK, BLK))
        down = jnp.transpose(across)
        for qi in range(kj, 4):
            ok = down == idr[0:1, BLK * qi : BLK * qi + BLK]
            if kj == qi:
                ok = ok & (
                    lax.broadcasted_iota(jnp.int32, (BLK, BLK), 0)
                    <= lax.broadcasted_iota(jnp.int32, (BLK, BLK), 1)
                )
            bias[block_at(qi, kj)] = jnp.where(ok, 0.0, -1e30)
    for i in range(1, 8):
        kk = group_peer(k, x, c, i)
        remote(vec, vec4.at[m, kk], vs.at[i - 1], vr.at[kk], (kk, x, c)).wait_recv()
    for i in (2, 3, 1):
        remote(vec4.at[m], vec4.at[m], vs2.at[i - 1], vr2.at[i - 1], unit_peer(k, x, c, i)).start()
    send_rows(gq.forward(1), wq)
    send_rows(gq.arrive(7), wq)
    wo_move.wait_recv()
    gox.start_y()
    send_rows(gq.forward(2), wq)
    send_rows(gq.forward(3), wq)
    go.start_z()
    gox.start_z()
    gf.start_z()
    gf.start_y()
    send_rows(gq.arrive(4), wq)
    for copy in own_in:
        copy.wait()
    gh.sibling()
    for i in (1, 2, 3):
        mm = 2 * (1 - x if i & 2 else x) + (1 - c if i & 1 else c)
        remote(vec4.at[mm], vec4.at[mm], vs2.at[i - 1], vr2.at[i - 1], unit_peer(k, x, c, i)).wait_recv()
    vectors_out(vec4, gv)

    def ln1(b):
        def body(i, carry):
            at_ = rows(BLK * b + 64 * i, 64)
            cc, r = centred(hall[at_, :].astype(F32))
            hat[at_, :] = cc * r
            norm[at_, :] = (cc * r * gv[0:1, :] + gv[1:2, :]).astype(BF)
            return carry
        lax.fori_loop(0, 4, body, 0)

    gh.forward()
    send_rows(gq.arrive(5), wq)
    ln1(m)
    go.forward(1)
    send_rows(gq.arrive(6), wq)
    gc[0].start(cot.at[0:HALF])
    ln1(2 * x + 1 - c)
    go.forward(2)
    go.forward(3)
    ln1(2 * (1 - x) + c)
    gh.finish()
    for i in (1, 2, 3):
        gox.forward(i)
    ln1(2 * (1 - x) + 1 - c)
    gp.start_z()
    gp.start_y()

    def take_rows(b, carry):
        blk = wqh.at[rows(24 * b, 24)]
        pltpu.make_async_copy(blk, blk, ur.at[b]).wait()
        return carry
    lax.fori_loop(0, 24, take_rows, 0)
    gq.own()

    def project(b, carry):
        sl = rows(BLK * b, BLK)
        qt[:, cols(BLK * b, BLK)] = nt(wqh[...], norm[sl, :]).astype(BF)
        return carry
    lax.fori_loop(0, 4, project, 0)

    gf.forward(1)
    pairs = ((m, 2 * x + 1 - c), (2 * (1 - x) + c, 2 * (1 - x) + 1 - c))
    wo_core = []

    def give(h, to):
        src = ot.at[HEAD * h : HEAD * h + HEAD, BLK * to : BLK * to + BLK]
        dst = at.at[rows(192 * m + HEAD * h, HEAD)]

        @pl.when(m == to)
        def _():
            dst[...] = src[...]

        @pl.when(m != to)
        def _():
            remote(src, dst, as_.at[4 * h + to], ar.at[4 * h + m], (k, to // 2, to % 2)).start()

    for h in range(3):
        attention_head(h, qt, bias, s_ref, e_ref, ot, inv_ref, give)
        if h == 0:
            go.finish()
            gox.finish()
            for i, (mine, _) in enumerate(pairs):
                copy = remote(wo4.at[:, mine], wo4.at[:, mine], gw_s.at[i], gw_r.at[i], sib)
                copy.start()
                wo_core.append(copy)
            gf.forward(2)
    gc[1].start(cot.at[HALF : 2 * HALF])
    gf.forward(3)
    gp.forward(1)
    for i, (_, other) in enumerate(pairs):
        blk = wo4.at[:, other]
        remote(blk, blk, gw_s.at[i], gw_r.at[i], sib).wait_recv()
    for d in range(32):
        wo[24 * d : 24 * d + 24, :] = wo4[d // 4, d % 4]
    gc[0].sibling()
    gc[0].forward()
    for h in range(3):
        for i in (1, 2, 3):
            dev = unit_peer(k, x, c, i)
            blk = at.at[rows(192 * (2 * dev[1] + dev[2]) + HEAD * h, HEAD)]
            remote(blk, blk, as_.at[0], ar.at[4 * h + 2 * dev[1] + dev[2]], dev).wait_recv()
    mid[...] = hall[rows(BLK * m, BLK), :].astype(F32) + tn(at[...], wo[...])
    for h in range(2):
        def ln2(i, carry):
            cc, r = centred(mid[rows(HALF * h + 64 * i, 64), :])
            to = 512 * x + 256 * h + HALF * c + 64 * i
            n2[rows(to, 64), :] = (cc * r * gv[2:3, :] + gv[3:4, :]).astype(BF)
            return carry
        lax.fori_loop(0, 2, ln2, 0)
        gn[h].start()
    gg[...] = jnp.zeros((8, D), F32)
    gp.forward(2)
    gf.finish()
    gp.forward(3)

    def chunk_of(it):
        pr, h = it // 2, lax.rem(it, 2)
        return rows(512 * flip(x, pr) + 256 * h, 256)

    def into_hidden(sl):
        u = nt(n2[sl, :], fc[...]) + gv[12:13, :]
        th = jnp.tanh(0.7978845608028654 * (u + 0.044715 * u * u * u))
        act[sl, :] = (0.5 * u * (1.0 + th)).astype(BF)
        slope[sl, :] = 0.5 * (1.0 + th) + 0.5 * u * (1.0 - th * th) * (
            0.7978845608028654 * (1.0 + 3.0 * 0.044715 * u * u)
        )

    def out_of_hidden(sl):
        d = (nt(call[sl, :], pj[...]) * slope[sl, :]).astype(BF)
        db[sl, :] = d
        gg[4:5, :] = gg[4:5, :] + jnp.sum(d.astype(F32), axis=0, keepdims=True)
        part[...] = nn(db[sl, :], fc[...])

    def near_in(j, carry):
        for h in range(2):
            @pl.when(j == h)
            def _():
                gn[h].sibling()
        into_hidden(chunk_of(j))
        return carry

    lax.fori_loop(0, 2, near_in, 0)
    for g in [gq, go, gox, gh, gf] + gc[:1]:
        g.drain()
    def drain_wq(b, carry):
        for j in range(3):
            g, slot = unit_of(b, j)

            @pl.when(g != m)
            def _():
                blk = wqh.at[0:24]
                remote(blk, blk, us.at[3 * b + j], ur.at[0], (k, g // 2, lax.rem(g, 2))).wait_send()
        return carry
    lax.fori_loop(0, 8, drain_wq, 0)
    for to in range(4):
        @pl.when(m != to)
        def _():
            blk = ot.at[0:HEAD, 0:BLK]
            for h in range(3):
                remote(blk, blk, as_.at[4 * h + to], ar.at[0], sib).wait_send()
    for copy in wo_core:
        copy.wait_send()
    wo_move.wait_send()
    for i in range(7):
        remote(vec, vec, vs.at[i], vr.at[0], sib).wait_send()
    for i in range(3):
        remote(vec4.at[m], vec4.at[m], vs2.at[i], vr2.at[0], sib).wait_send()
    gc[0].finish()

    def near_out(j, carry):
        out_of_hidden(chunk_of(j))

        @pl.when(j == 0)
        def _():
            rs_pj.pass_on(1)
        for h in range(2):
            @pl.when(j == h)
            def _():
                red_mid[h].give_own(part[rows(HALF * (1 - c), HALF), :])
                dmid[HALF * h : HALF * h + HALF, :] = part[rows(HALF * c, HALF), :]
        return carry

    def far_in(j, carry):
        for h in range(2):
            @pl.when(j == h)
            def _():
                gn[h].forward()
                gn[h].finish()
        into_hidden(chunk_of(2 + j))
        return carry

    def far_out(j, carry):
        out_of_hidden(chunk_of(2 + j))
        for h in range(2):
            @pl.when(j == h)
            def _():
                red_mid[h].give_far(part[rows(HALF * (1 - c), HALF), :])
                far_part[h] = part[rows(HALF * c, HALF), :]
        return carry

    def grads_pj(j, carry):
        at_ = 384 * jnp.where(k < 4, 1 - j, j)
        gs_pj[rows(at_, 384), :] = tn(act[:, cols(at_, 384)], call[...]).astype(BF)
        for half in range(2):
            @pl.when(j == half)
            def _():
                rs_pj.start(half)
        return carry

    gc[1].sibling()
    gc[1].forward()
    lax.fori_loop(0, 2, far_in, 0)
    gc[1].finish()
    lax.fori_loop(0, 2, grads_pj, 0)
    gp.finish()
    lax.fori_loop(0, 2, far_out, 0)
    red_mid[0].cross(far_part[0])
    red_mid[1].cross(far_part[1])
    lax.fori_loop(0, 2, near_out, 0)

    def grads_fc(j, carry):
        at_ = 384 * jnp.where(k < 4, 1 - j, j)
        gs_fc[rows(at_, 384), :] = tn(db[:, cols(at_, 384)], n2[...]).astype(BF)
        for half in range(2):
            @pl.when(j == half)
            def _():
                rs_fc.start(half)
        return carry
    lax.fori_loop(0, 2, grads_fc, 0)
    rs_pj.pass_on(2)

    def block_sum(it, carry):
        part[...] = nn(act[chunk_of(it), :], pj[...])
        for h in range(2):
            @pl.when(it == h)
            def _():
                red_out[h].give_own(part[rows(HALF * (1 - c), HALF), :])
                hh = slice(HALF * h, HALF * h + HALF)
                mid_out[hh, :] = mid[hh, :] + part[rows(HALF * c, HALF), :]

            @pl.when(it == 2 + h)
            def _():
                red_out[h].give_far(part[rows(HALF * (1 - c), HALF), :])
                far_part[h] = part[rows(HALF * c, HALF), :]
        return carry

    lax.fori_loop(0, 4, block_sum, 0)
    for h in range(2):
        red_mid[h].arrive()

        def ln2_back(i, carry):
            sl = rows(HALF * h + 64 * i, 64)
            grad = dmid[sl, :] + red_mid[h].rest(rows(64 * i, 64))
            back, unit = norm_back(mid[sl, :], gv[2:3, :], grad)
            g = call[rows(512 * x + 256 * h + HALF * c + 64 * i, 64), :].astype(F32) + back
            dmid[sl, :] = g
            mlow[sl, :] = g.astype(BF)
            gg[2:3, :] = gg[2:3, :] + jnp.sum(grad * unit, axis=0, keepdims=True)
            gg[3:4, :] = gg[3:4, :] + jnp.sum(grad, axis=0, keepdims=True)
            return carry
        lax.fori_loop(0, 2, ln2_back, 0)
    agt[...] = nt(wo[...], mlow[...]).astype(BF)
    for h in range(3):
        for i in (2, 3, 1):
            dev = unit_peer(k, x, c, i)
            to = 2 * dev[1] + dev[2]
            remote(
                agt.at[rows(192 * to + HEAD * h, HEAD)],
                dot.at[HEAD * h : HEAD * h + HEAD, cols(BLK * m, BLK)],
                ds_.at[3 * h + i - 1], dr_.at[3 * h + i - 1], dev,
            ).start()
        dot[HEAD * h : HEAD * h + HEAD, cols(BLK * m, BLK)] = agt[rows(192 * m + HEAD * h, HEAD), :]
    red_out[0].cross(far_part[0])
    gout = nn(at[...], mlow[...])
    for d in range(32):
        go4[d // 4, d % 4] = gout[24 * d : 24 * d + 24, :].astype(BF)
    core_a = remote(go4.at[:, 2 * x + 1 - c], go_r.at[0], go_s_sem.at[0], go_r_sem.at[0], sib)
    core_b = remote(go4.at[:, 2 * (1 - x) + 1 - c], go_r.at[1], go_s_sem.at[1], go_r_sem.at[1], sib)
    core_a.start()
    core_b.start()
    rs_pj.pass_on(3)
    rs_fc.pass_on(1)

    def give_rows(lo, hi):
        def body(w, carry):
            for p in range(3):
                u = 32 * p + 8 * m + w
                b, j, to = u // 12, lax.rem(u, 3), lax.rem(u // 3, 4)
                src = gh_q.at[rows(24 * (8 * p + w), 24)]
                dst = gsw.at[rows(24 * (8 * j + 4 * lax.rem(b, 2) + b // 2), 24)]

                @pl.when(to == m)
                def _():
                    pltpu.make_async_copy(src, dst, xr.at[3 * b + j]).start()

                @pl.when(to != m)
                def _():
                    remote(
                        src, dst, xs.at[8 * p + w], xr.at[3 * b + j], (k, to // 2, lax.rem(to, 2))
                    ).start()
            return carry
        lax.fori_loop(lo, hi, body, 0)

    def drain_rows():
        def body(w, carry):
            for p in range(3):
                u = 32 * p + 8 * m + w
                to = lax.rem(u // 3, 4)
                src = gh_q.at[rows(24 * (8 * p + w), 24)]

                @pl.when(to != m)
                def _():
                    remote(
                        src, src, xs.at[8 * p + w], xr.at[0], (k, to // 2, lax.rem(to, 2))
                    ).wait_send()
            return carry
        lax.fori_loop(0, 8, body, 0)

    z, y = k // 2, lax.rem(k, 2)
    y_dev = (2 * z + 1 - y, x, c)

    def rows_over_y(lo, hi):
        def body(w, carry):
            j, e = units_of(m, w)

            @pl.when(j < 3)
            def _():
                for zz in range(4):
                    b = 2 * zz + e
                    blk = gsw.at[rows(24 * (8 * j + 4 * e + zz), 24)]
                    pltpu.make_async_copy(blk, blk, xr.at[3 * b + j]).wait()

                @pl.when(e != y)
                def _():
                    remote(
                        gsw.at[rows(24 * (8 * j + 4 * e), 96)], gsy.at[rows(96 * j, 96)],
                        sy_wq.at[j], ry_wq.at[j], y_dev,
                    ).start()
            return carry
        lax.fori_loop(lo, hi, body, 0)

    def rows_over_z(lo, hi):
        def body(w, carry):
            j, e = units_of(m, w)

            @pl.when((j < 3) & (e == y))
            def _():
                blk = gsy.at[rows(96 * j, 96)]
                remote(blk, blk, sy_wq.at[j], ry_wq.at[j], y_dev).wait_recv()
                base = 24 * (8 * j + 4 * e)
                gsz[rows(96 * j, 96), :] = (
                    gsw[rows(base, 96), :].astype(F32) + gsy[rows(96 * j, 96), :].astype(F32)
                ).astype(BF)
                for i in (3, 2, 1):
                    kk = group_peer(k, x, c, i)
                    remote(
                        gsz.at[rows(96 * j + 24 * (kk // 2), 24)], gsr.at[rows(96 * j + 24 * z, 24)],
                        sz_wq.at[j, i - 1], rz_wq.at[j, z], (kk, x, c),
                    ).start()
            return carry
        lax.fori_loop(lo, hi, body, 0)

    def rows_done():
        for j in range(3):
            total = gsw[rows(24 * (8 * j + 4 * y + z), 24), :].astype(F32)
            total = total + gsy[rows(96 * j + 24 * z, 24), :].astype(F32)
            for i in (1, 2, 3):
                zz = group_peer(k, x, c, i) // 2
                blk = gsr.at[rows(96 * j + 24 * zz, 24)]
                remote(blk, blk, sz_wq.at[j, 0], rz_wq.at[j, zz], y_dev).wait_recv()
                total = total + gsr[rows(96 * j + 24 * zz, 24), :].astype(F32)
            g_wq[24 * j : 24 * j + 24, :] = total

    def await_head(h):
        for i in (1, 2, 3):
            dev = unit_peer(k, x, c, i)
            blk = dot.at[HEAD * h : HEAD * h + HEAD, cols(BLK * (2 * dev[1] + dev[2]), BLK)]
            remote(blk, blk, ds_.at[0], dr_.at[3 * h + i - 1], dev).wait_recv()

    def head_grads(h):
        lo = HEAD * h
        three = jnp.concatenate([pgt[192 * p + lo : 192 * p + lo + HEAD, :] for p in range(3)], axis=0)
        res = nn(three, norm[...])
        for p in range(3):
            gh_q[192 * p + lo : 192 * p + lo + HEAD, :] = res[HEAD * p : HEAD * p + HEAD, :].astype(BF)

    await_head(0)
    attention_back(0, qt, dot, e_ref, inv_ref, s_ref, dk, dv, pgt)
    head_grads(0)
    give_rows(0, 2)
    rs_fc.pass_on(2)
    core_a.wait_recv()
    core_b.wait_recv()
    for part_of, (own, _) in enumerate(pairs):
        both = go4[:, own].astype(F32) + go_r[part_of].astype(F32)
        for kk in range(8):
            gs_wo[48 * kk + 24 * part_of : 48 * kk + 24 * part_of + 24, :] = both[kk].astype(BF)
    rs_wo.start(0)
    rs_wo.start(1)
    await_head(1)
    attention_back(1, qt, dot, e_ref, inv_ref, s_ref, dk, dv, pgt)
    head_grads(1)
    give_rows(2, 5)
    rs_fc.pass_on(3)
    await_head(2)
    attention_back(2, qt, dot, e_ref, inv_ref, s_ref, dk, dv, pgt)
    head_grads(2)
    give_rows(5, 8)

    def place_in(b0, far_side, h):
        to = 2 * (1 - x if far_side else x) + (1 - c if b0 else c)
        return BLK * to + HALF * h

    def back_in(b0, far_side, h):
        at_ = place_in(b0, far_side, h)
        slope[rows(at_, HALF), :] = tn(pgt[:, cols(at_, HALF)], wqh[...])
        return slope[rows(at_, HALF), :]

    rows_over_y(0, 2)
    rs_wo.pass_on(1)
    for h in range(2):
        red_in[h].give_far(back_in(1, True, h))
    for h in range(2):
        back_in(0, True, h)
    rows_over_y(2, 5)
    rs_wo.pass_on(2)
    for h in range(2):
        red_in[h].give_own(back_in(1, False, h))
        back_in(0, False, h)

    def ln1_sums(i, carry):
        sl = rows(64 * i, 64)
        v = slope[sl, :]
        gg[0:1, :] = gg[0:1, :] + jnp.sum(v * hat[sl, :], axis=0, keepdims=True)
        gg[1:2, :] = gg[1:2, :] + jnp.sum(v, axis=0, keepdims=True)
        return carry
    lax.fori_loop(0, 16, ln1_sums, 0)
    for i in (2, 3, 1):
        remote(gg, ex_r.at[i - 1], es.at[i - 1], er.at[i - 1], unit_peer(k, x, c, i)).start()
    for h in range(2):
        red_in[h].cross(slope[rows(place_in(0, True, h), HALF), :])
    red_out[1].cross(far_part[1])
    rows_over_y(5, 8)
    rs_wo.pass_on(3)
    rows_over_z(0, 2)
    lane = lane_div(D, 24)
    lane_fc = lane_div(D, 96)
    row = lax.broadcasted_iota(jnp.int32, (8, D), 0)
    total = jnp.where(row < 4, gg[...], 0.0)
    for i in (1, 2, 3):
        dev = unit_peer(k, x, c, i)
        remote(ex_r.at[i - 1], ex_r.at[i - 1], es.at[0], er.at[i - 1], dev).wait_recv()
        total = total + jnp.where(row < 4, ex_r[i - 1], 0.0)
    five = jnp.where(row == 4, gg[...], 0.0)
    for kk in range(8):
        wide[8 * kk : 8 * kk + 8, :] = jnp.where(lane == 4 * kk + m, total, 0.0)
        wide[64 + 8 * kk : 72 + 8 * kk, :] = jnp.where(lane_fc == kk, five, 0.0)
    ex_m[...] = nt_two(wide[0:64, :], spread(24)) + nt_two(wide[64:128, :], spread(96))
    for i in range(1, 8):
        kk = group_peer(k, x, c, i)
        remote(ex_m.at[rows(8 * kk, 8)], ex_g.at[k], es2.at[i - 1], er2.at[k], (kk, x, c)).start()
    rows_over_z(2, 5)
    rs_pj.finish(g_pj)
    rs_fc.finish(g_fc)
    for g in [gp, gc[1]] + gn + red_mid + [rs_pj]:
        g.drain()
    rows_over_z(5, 8)
    rs_wo.finish(w48)
    wo_out[...] = w48[24:48, :].astype(BF)
    cross = remote(wo_out, go_x, go_s_sem.at[2], go_r_sem.at[2], far)
    cross.start()
    for h in range(2):
        red_in[h].arrive()

        def ln1_back(i, carry):
            sl = rows(HALF * h + 64 * i, 64)
            grad = slope[rows(place_in(0, False, h) + 64 * i, 64), :] + red_in[h].rest(rows(64 * i, 64))
            back, _ = norm_back(hall[rows(BLK * m + HALF * h + 64 * i, 64), :].astype(F32), gv[0:1, :], grad)
            in_grad[sl, :] = (dmid[sl, :] + back).astype(BF)
            return carry
        lax.fori_loop(0, 2, ln1_back, 0)
    rows_done()
    for h in range(2):
        red_out[h].arrive()
        hh = slice(HALF * h, HALF * h + HALF)
        block_out[hh, :] = (mid_out[hh, :] + red_out[h].rest(slice(None))).astype(BF)
    last = ex_m[rows(8 * k, 8), :]
    for i in range(1, 8):
        kk = group_peer(k, x, c, i)
        remote(ex_g.at[kk], ex_g.at[kk], es2.at[0], er2.at[kk], (kk, x, c)).wait_recv()
        last = last + ex_g[kk]
    o_vec[...] = last
    cross.wait_recv()
    g_wo[...] = w48[0:24, :] + go_x[...].astype(F32)
    for g in [rs_fc, rs_wo] + red_out + red_in:
        g.drain()

    drain_rows()
    for h in range(3):
        for i in (1, 2, 3):
            blk = ot.at[HEAD * h : HEAD * h + HEAD, 0:BLK]
            remote(blk, blk, ds_.at[3 * h + i - 1], dr_.at[0], unit_peer(k, x, c, i)).wait_send()
    for j in range(3):
        blk = gsy.at[0:96]
        remote(blk, blk, sy_wq.at[j], ry_wq.at[0], y_dev).wait_send()
        for i in range(3):
            blk = gsz.at[0:24]
            remote(blk, blk, sz_wq.at[j, i], rz_wq.at[0, 0], y_dev).wait_send()
    core_a.wait_send()
    core_b.wait_send()
    cross.wait_send()
    for i in range(7):
        remote(ex_g.at[0], ex_g.at[0], es2.at[i], er2.at[0], sib).wait_send()
    for i in range(3):
        remote(gg, gg, es.at[i], er.at[0], sib).wait_send()


def layer_call(*operands):
    dma = pltpu.SemaphoreType.DMA
    vm = pl.BlockSpec(memory_space=pltpu.VMEM)
    here = pl.BlockSpec(memory_space=pl.ANY)
    out_shape = [
        jax.ShapeDtypeStruct(s, t)
        for s, t in (
            ((256, D), BF), ((256, D), BF), ((72, D), F32), ((24, D), F32), ((96, D), F32), ((96, D), F32),
            ((8, 128), F32),
        )
    ]
    return pl.pallas_call(
        layer_kernel,
        out_shape=out_shape,
        in_specs=[here] * 2 + [vm] * 6 + [here] * 4,
        out_specs=[vm] * len(out_shape),
        scratch_shapes=[
            pltpu.VMEM((256, D), F32), pltpu.VMEM((1024, D), BF), pltpu.VMEM((1024, D), BF),
            pltpu.VMEM((1024, D), BF), pltpu.VMEM((576, D), BF), pltpu.VMEM((576, D), BF),
            pltpu.VMEM((D, D), BF), pltpu.VMEM((D, D), BF), pltpu.VMEM((D, D), BF),
            pltpu.VMEM((576, 1024), BF), pltpu.VMEM((D, 256), BF), pltpu.VMEM((3, 1, 1024), F32),
            pltpu.VMEM((192, 1024), BF), pltpu.VMEM((16, D), F32), pltpu.VMEM((10, BLK, BLK), F32),
            pltpu.VMEM((8, 1024), F32), pltpu.VMEM((3, 10, BLK, BLK), BF),
            pltpu.VMEM((1024, D), F32), pltpu.VMEM((4, 8, 8, 128), BF), pltpu.VMEM((8, 128), F32),
            pltpu.VMEM((8, 128), BF), pltpu.VMEM((1024, D), BF), pltpu.VMEM((1024, 256), F32),
            pltpu.VMEM((64, 1024), F32), pltpu.VMEM((64, 1024), F32), pltpu.VMEM((1024, D), BF),
            pltpu.VMEM((1024, D), BF), pltpu.VMEM((1024, D), F32), pltpu.VMEM((256, D), F32),
            pltpu.VMEM((256, D), F32), pltpu.VMEM((2, 128, D), F32), pltpu.VMEM((256, D), F32),
            pltpu.VMEM((256, D), BF), pltpu.VMEM((D, 256), BF), pltpu.VMEM((192, 1024), BF),
            pltpu.VMEM((576, 1024), BF), pltpu.VMEM((8, D), F32), pltpu.VMEM((D, D), BF),
            pltpu.VMEM((D, D), BF), pltpu.VMEM((384, D), BF), pltpu.VMEM((48, D), F32),
            pltpu.VMEM((24, D), BF), pltpu.VMEM((576, D), BF), pltpu.VMEM((576, D), BF),
            pltpu.VMEM((288, D), BF), pltpu.VMEM((288, D), BF), pltpu.VMEM((288, D), BF),
            pltpu.VMEM((2, 6, 128, D), BF), pltpu.VMEM((2, 6, 128, D), BF),
            pltpu.VMEM((2, 6, 128, D), BF), pltpu.VMEM((8, 4, 24, D), BF),
            pltpu.VMEM((2, 8, 24, D), BF), pltpu.VMEM((24, D), BF), pltpu.VMEM((8, 4, 24, D), BF),
            pltpu.VMEM((24, D), BF), pltpu.VMEM((128, D), F32), pltpu.VMEM((3, 8, D), F32),
            pltpu.VMEM((64, 128), F32), pltpu.VMEM((8, 8, 128), F32), pltpu.VMEM((384, D), BF),
            pltpu.VMEM((384, D), BF), pltpu.VMEM((384, D), BF), pltpu.VMEM((96, D), BF), dma((1,)),
            dma((4,)), dma((4,)), dma((3,)), dma((4,)), pltpu.VMEM((384, D), BF),
            pltpu.VMEM((384, D), BF), pltpu.VMEM((384, D), BF), pltpu.VMEM((96, D), BF), dma((1,)),
            dma((4,)), dma((4,)), dma((3,)), dma((4,)), pltpu.VMEM((192, D), BF),
            pltpu.VMEM((192, D), BF), pltpu.VMEM((192, D), BF), pltpu.VMEM((48, D), BF), dma((1,)),
            dma((4,)), dma((4,)), dma((3,)), dma((4,)), dma((3,)), dma((3,)), dma((3, 3)),
            dma((3, 4)), dma((7,)), dma((8,)), dma((3,)), dma((3,)), dma((3,)), dma((3,)),
            dma((8,)), dma((8,)), dma((8,)), dma((8,)), dma((8,)), dma((8,)), dma((8,)), dma((8,)),
            dma((24,)), dma((24,)), dma((2, 3)), dma((2, 3)), dma((2, 3)), dma((2, 3)),
            dma((2, 3)), dma((2, 3)), dma((2, 3)), dma((2, 3)), dma((2, 3)), dma((2, 3)),
            dma((12,)), dma((12,)), dma((5,)), dma((3,)), dma((8,)), dma((8,)), dma((1,)),
            dma((1,)), dma((2,)), dma((2,)), dma((9,)), dma((9,)), dma((24,)), dma((24,)),
            dma((3,)), dma((3,)), dma((3,)), dma((3,)), dma((7,)), dma((8,)),
        ],
        compiler_params=pltpu.CompilerParams(
            collective_id=0, has_side_effects=True, vmem_limit_bytes=63 * 1024 * 1024
        ),
        name="layer",
    )(*operands)


def hand_over(*refs):
    blocks, tile, outs = refs[:6], refs[6], refs[7:]
    for src, dst in zip(blocks, outs[:6]):
        dst[...] = src[...]
    for i in range(4):
        outs[6 + i][...] = tile[i : i + 1, 0:24]
    outs[10][...] = tile[4:5, 0:96]


def hand_over_call(*results):
    vm = pl.BlockSpec(memory_space=pltpu.VMEM)
    shapes = [jax.ShapeDtypeStruct(r.shape, r.dtype) for r in results[:6]]
    shapes += [jax.ShapeDtypeStruct((1, 24), F32)] * 4 + [jax.ShapeDtypeStruct((1, 96), F32)]
    return pl.pallas_call(
        hand_over,
        out_shape=shapes,
        in_specs=[vm] * 7,
        out_specs=[vm] * 11,
        name="hand_over",
    )(*results)


def fused_on_device(
    hidden_in,
    clip_id,
    w_qkv,
    w_out,
    w_fc,
    w_proj,
    ln1_gain,
    ln1_bias,
    ln2_gain,
    ln2_bias,
    fc_bias,
    cotangent,
):
    tok_rows = hidden_in.shape[2]
    results = layer_call(
        hidden_in.reshape(tok_rows, -1),
        cotangent.reshape(tok_rows, -1),
        clip_id[0],
        *(v.reshape(1, -1) for v in (ln1_gain, ln1_bias, ln2_gain, ln2_bias, fc_bias)),
        w_qkv.T,
        w_out,
        w_fc.T,
        w_proj,
    )
    results = hand_over_call(*results)
    block_out, input_grad, grad_qkv, grad_out, grad_fc, grad_proj = results[:6]
    return (
        block_out.reshape(hidden_in.shape),
        input_grad.reshape(hidden_in.shape),
        grad_qkv.T,
        grad_out,
        grad_fc.T,
        grad_proj,
    ) + tuple(v.reshape(-1) for v in results[6:])


def on_device(
    hidden_in,
    clip_id,
    w_qkv,
    w_out,
    w_fc,
    w_proj,
    ln1_gain,
    ln1_bias,
    ln2_gain,
    ln2_bias,
    fc_bias,
    cotangent,
):
    weights = (
        lax.all_gather(w_qkv, ("seq", "cf", "fsdp"), axis=1, tiled=True),
        lax.all_gather(w_out, ("seq", "cf", "fsdp"), axis=0, tiled=True),
        lax.all_gather(w_fc, ("seq", "cf", "fsdp"), axis=1, tiled=True),
        lax.all_gather(w_proj, ("seq", "cf", "fsdp"), axis=0, tiled=True),
        lax.all_gather(ln1_gain, ("seq", "cf", "fsdp"), axis=0, tiled=True),
        lax.all_gather(ln1_bias, ("seq", "cf", "fsdp"), axis=0, tiled=True),
        lax.all_gather(ln2_gain, ("seq", "cf", "fsdp"), axis=0, tiled=True),
        lax.all_gather(ln2_bias, ("seq", "cf", "fsdp"), axis=0, tiled=True),
        lax.all_gather(fc_bias, ("seq", "cf", "fsdp"), axis=0, tiled=True),
    )
    tok_rows = hidden_in.shape[2]
    source = hidden_in.reshape(tok_rows, -1).astype(jnp.float32)
    allowed = key_masks(clip_id, tok_rows)
    saved = forward_core(source, weights, allowed)
    block_out = (
        (saved[5] + plain_dot(saved[8], weights[3])).astype(jnp.bfloat16).reshape(hidden_in.shape)
    )
    weights = (
        lax.all_gather(w_qkv, ("seq", "cf", "fsdp"), axis=1, tiled=True),
        lax.all_gather(w_out, ("seq", "cf", "fsdp"), axis=0, tiled=True),
        lax.all_gather(w_fc, ("seq", "cf", "fsdp"), axis=1, tiled=True),
        lax.all_gather(w_proj, ("seq", "cf", "fsdp"), axis=0, tiled=True),
        lax.all_gather(ln1_gain, ("seq", "cf", "fsdp"), axis=0, tiled=True),
        lax.all_gather(ln1_bias, ("seq", "cf", "fsdp"), axis=0, tiled=True),
        lax.all_gather(ln2_gain, ("seq", "cf", "fsdp"), axis=0, tiled=True),
        lax.all_gather(ln2_bias, ("seq", "cf", "fsdp"), axis=0, tiled=True),
        lax.all_gather(fc_bias, ("seq", "cf", "fsdp"), axis=0, tiled=True),
    )
    saved = forward_core(source, weights, allowed)
    normed, packed, attended, log_total, key_rows, middle, normed_two, before, activated = saved
    (
        weight_qkv,
        weight_out,
        weight_fc,
        weight_proj,
        gain_one,
        bias_one,
        gain_two,
        bias_two,
        fc_shift,
    ) = weights
    out_grad = cotangent.reshape(tok_rows, -1)
    grad_proj = inner_dot(activated, out_grad)
    _, gelu_back = jax.vjp(gelu_tanh, before)
    before_grad = gelu_back(outer_dot(out_grad, weight_proj))[0].astype(jnp.bfloat16)
    grad_shift = jnp.sum(before_grad, axis=0, dtype=jnp.float32)
    grad_fc = inner_dot(normed_two, before_grad)
    _, norm_two_back = jax.vjp(
        norm_rows, middle, gain_two.astype(jnp.float32), bias_two.astype(jnp.float32)
    )
    middle_part, grad_gain_two, grad_bias_two = norm_two_back(outer_dot(before_grad, weight_fc))
    middle_grad = out_grad.astype(jnp.float32) + middle_part
    middle_low = middle_grad.astype(jnp.bfloat16)
    grad_out = inner_dot(attended, middle_low)
    attended_grad = outer_dot(middle_low, weight_out).astype(jnp.bfloat16)
    query_grad, key_value_grad = attend_back(packed, key_rows, log_total, attended_grad, allowed)
    half_rows = key_value_grad.shape[0] // 2
    returned = from_behind(key_value_grad[:half_rows].astype(jnp.bfloat16), "cf", -1).astype(
        jnp.float32
    )
    owned = lax.psum_scatter(
        (key_value_grad[half_rows:] + returned).astype(jnp.bfloat16),
        "fsdp",
        scatter_dimension=0,
        tiled=True,
    ).astype(jnp.float32)
    packed_grad = jnp.concatenate([query_grad, owned], axis=1).astype(jnp.bfloat16)
    grad_qkv = inner_dot(normed, packed_grad)
    _, norm_one_back = jax.vjp(
        norm_rows, source, gain_one.astype(jnp.float32), bias_one.astype(jnp.float32)
    )
    source_part, grad_gain_one, grad_bias_one = norm_one_back(outer_dot(packed_grad, weight_qkv))
    input_grad = (middle_grad + source_part).astype(jnp.bfloat16).reshape(hidden_in.shape)
    col_grads = (grad_qkv, grad_fc)
    row_grads = (
        grad_out,
        grad_proj,
        grad_gain_one,
        grad_bias_one,
        grad_gain_two,
        grad_bias_two,
        grad_shift,
    )
    outer_count = lax.axis_size(("seq", "cf"))
    inner_count = lax.axis_size("fsdp")
    col_split = tuple((split_dim(grad, 1, outer_count, inner_count) for grad in col_grads))
    row_split = tuple((split_dim(grad, 0, outer_count, inner_count) for grad in row_grads))
    col_moved = (
        lax.all_to_all(
            col_split[0].astype(jnp.bfloat16), "fsdp", split_axis=2, concat_axis=2, tiled=True
        ).astype(jnp.float32),
        lax.all_to_all(
            col_split[1].astype(jnp.bfloat16), "fsdp", split_axis=2, concat_axis=2, tiled=True
        ).astype(jnp.float32),
    )
    row_moved = (
        lax.all_to_all(
            row_split[0].astype(jnp.bfloat16), "fsdp", split_axis=1, concat_axis=1, tiled=True
        ).astype(jnp.float32),
        lax.all_to_all(
            row_split[1].astype(jnp.bfloat16), "fsdp", split_axis=1, concat_axis=1, tiled=True
        ).astype(jnp.float32),
        lax.all_to_all(
            row_split[2].astype(jnp.bfloat16), "fsdp", split_axis=1, concat_axis=1, tiled=True
        ).astype(jnp.float32),
        lax.all_to_all(
            row_split[3].astype(jnp.bfloat16), "fsdp", split_axis=1, concat_axis=1, tiled=True
        ).astype(jnp.float32),
        lax.all_to_all(
            row_split[4].astype(jnp.bfloat16), "fsdp", split_axis=1, concat_axis=1, tiled=True
        ).astype(jnp.float32),
        lax.all_to_all(
            row_split[5].astype(jnp.bfloat16), "fsdp", split_axis=1, concat_axis=1, tiled=True
        ).astype(jnp.float32),
        lax.all_to_all(
            row_split[6].astype(jnp.bfloat16), "fsdp", split_axis=1, concat_axis=1, tiled=True
        ).astype(jnp.float32),
    )
    col_near = tuple((jnp.sum(part, axis=2) for part in col_moved))
    row_near = tuple((jnp.sum(part, axis=1) for part in row_moved))
    reduced = (
        lax.psum_scatter(col_near[0], ("seq", "cf"), scatter_dimension=1, tiled=True),
        lax.psum_scatter(col_near[1], ("seq", "cf"), scatter_dimension=1, tiled=True),
        lax.psum_scatter(row_near[0], ("seq", "cf"), scatter_dimension=0, tiled=True),
        lax.psum_scatter(row_near[1], ("seq", "cf"), scatter_dimension=0, tiled=True),
        lax.psum_scatter(row_near[2], ("seq", "cf"), scatter_dimension=0, tiled=True),
        lax.psum_scatter(row_near[3], ("seq", "cf"), scatter_dimension=0, tiled=True),
        lax.psum_scatter(row_near[4], ("seq", "cf"), scatter_dimension=0, tiled=True),
        lax.psum_scatter(row_near[5], ("seq", "cf"), scatter_dimension=0, tiled=True),
        lax.psum_scatter(row_near[6], ("seq", "cf"), scatter_dimension=0, tiled=True),
    )
    cols_done = tuple((merge_dims(part, 1) for part in reduced[:2]))
    rows_done = tuple((merge_dims(part, 0) for part in reduced[2:]))
    return (
        block_out,
        input_grad,
        cols_done[0],
        rows_done[0],
        cols_done[1],
        rows_done[1],
        rows_done[2],
        rows_done[3],
        rows_done[4],
        rows_done[5],
        rows_done[6],
    )


def solution(mesh):
    in_specs = (
        P("seq", "cf", "fsdp", None),
        P("seq", None, None),
        P(None, ("seq", "cf", "fsdp")),
        P(("seq", "cf", "fsdp"), None),
        P(None, ("seq", "cf", "fsdp")),
        P(("seq", "cf", "fsdp"), None),
        P(("seq", "cf", "fsdp")),
        P(("seq", "cf", "fsdp")),
        P(("seq", "cf", "fsdp")),
        P(("seq", "cf", "fsdp")),
        P(("seq", "cf", "fsdp")),
        P("seq", "cf", "fsdp", None),
    )
    out_specs = (
        P("seq", "cf", "fsdp", None),
        P("seq", "cf", "fsdp", None),
        P(None, ("seq", "cf", "fsdp")),
        P(("seq", "cf", "fsdp"), None),
        P(None, ("seq", "cf", "fsdp")),
        P(("seq", "cf", "fsdp"), None),
        P(("seq", "cf", "fsdp")),
        P(("seq", "cf", "fsdp")),
        P(("seq", "cf", "fsdp")),
        P(("seq", "cf", "fsdp")),
        P(("seq", "cf", "fsdp")),
    )
    local = fused_on_device if mesh.shape["seq"] == 8 else on_device
    return jax.shard_map(
        local, mesh=mesh, in_specs=in_specs, out_specs=out_specs, check_vma=False
    )
```
